32 devices in a mesh: row: 4 (over z), col: 8 (over y, x, core).
Axes of the slice: x: 2, y: 2, z: 4, core: 2. Of those that a mesh axis runs over, the one named last changes fastest.
Arguments:
- tokens: bfloat16 [512, 4096], P('row', 'col'), may hold values from -6 to 6
- cotangent: bfloat16 [512, 4096], P('row', 'col'), may hold values from -6 to 6
- gate_weight: bfloat16 [4096, 16384], P('row', 'col'), may hold values from -0.1875 to 0.1875
- up_weight: bfloat16 [4096, 16384], P('row', 'col'), may hold values from -0.1875 to 0.1875
- down_weight: bfloat16 [16384, 4096], P('col', 'row'), may hold values from -0.09375 to 0.09375
- gate_mask: int32 [32, 128], P('row', 'col'), may hold values from 0 to 1, as said below
- up_mask: int32 [32, 128], P('row', 'col'), may hold values from 0 to 1, as said below
- down_mask: int32 [128, 32], P('col', 'row'), may hold values from 0 to 1, as said below
Outputs:
- output: bfloat16 [512, 4096], P('row', 'col')
- grad_tokens: bfloat16 [512, 4096], P('row', 'col')
The draws below stay inside these ranges and needn't reach their ends.
Inputs may be any that keep to these rules, and one draw needn't show every extreme that they name: `gate_mask`: cut into aligned tiles of 8 x 16 entries (one device's shard), no tile holds more than 96 ones and some tile holds exactly 96. `up_mask`: cut into aligned tiles of 8 x 16 entries (one device's shard), no tile holds more than 96 ones and some tile holds exactly 96. `down_mask`: cut into aligned tiles of 16 x 8 entries (one device's shard), no tile holds more than 96 ones and some tile holds exactly 96.
All inputs are finite; a program needn't handle non-finite values.
Results may differ from the reference program's by a relative error of at most 0.015.
Values may be sent and summed in bfloat16 or wider, within the bound.
A program may use at most 192 MiB of HBM per device.

```python
import jax
import jax.numpy as jnp
from jax import lax

BLOCK = 128
D = 4096
FF = 16384
TOKENS = 512
CAP = 96
N_ROW = 4
N_COL = 8


def mask_draw(key, row_blocks, col_blocks, row_parts, col_parts):
    per_row = row_blocks // row_parts
    per_col = col_blocks // col_parts
    shard_count = row_parts * col_parts
    shard_blocks = per_row * per_col
    key_fullest, key_counts, key_order = jax.random.split(key, 3)
    fullest = jax.random.randint(key_fullest, (), 0, shard_count)
    counts = jax.random.randint(key_counts, (shard_count,), shard_blocks // 4, CAP + 1)
    counts = jnp.where(jnp.arange(shard_count) == fullest, CAP, counts)
    scores = jax.random.randint(key_order, (shard_count, shard_blocks), 0, 1 << 20)
    scores = scores * shard_blocks + jnp.arange(shard_blocks, dtype=jnp.int32)[None, :]
    rank_order = jnp.argsort(jnp.argsort(scores, axis=1), axis=1)
    kept_mask = (rank_order < counts[:, None]).astype(jnp.int32)
    kept_mask = kept_mask.reshape(row_parts, col_parts, per_row, per_col)
    kept_mask = kept_mask.transpose(0, 2, 1, 3).reshape(row_blocks, col_blocks)
    return kept_mask


def draw_gate_mask(key, part):
    return mask_draw(jax.random.fold_in(key, 11), D // BLOCK, FF // BLOCK, N_ROW, N_COL)


def draw_up_mask(key, part):
    return mask_draw(jax.random.fold_in(key, 23), D // BLOCK, FF // BLOCK, N_ROW, N_COL)


def draw_down_mask(key, part):
    return mask_draw(jax.random.fold_in(key, 37), FF // BLOCK, D // BLOCK, N_COL, N_ROW)


def spiked(result, own_key, source, target, parts, factor):
    owner, partner = [(jnp.arange(result.shape[dim]) // (result.shape[dim] // parts)).reshape([-1 if axis == dim else 1 for axis in range(result.ndim)]) for dim in (source, target)]
    chosen = jax.random.permutation(own_key, parts)[partner]
    strong = (owner == chosen) | (owner == (partner + parts // 2) % parts)
    return jnp.where(strong, factor * result, result)


def block_scale(stream_key, dims, cuts, least, high):
    level, own = 1.0, jax.random.fold_in(stream_key, 6)
    for position, parts in cuts:
        draws = jnp.exp(jax.random.uniform(jax.random.fold_in(own, position), (parts,), jnp.float32, least / len(cuts), high / len(cuts)))
        level = level * jnp.repeat(draws, dims[position] // parts).reshape([-1 if axis == position else 1 for axis in range(len(dims))])
    return level


def noise(rng, extent, scale, most, shards=(), held_as=jnp.bfloat16):
    drawn = scale * jax.random.normal(rng, extent, jnp.float32)
    if shards:
        drawn = drawn * block_scale(rng, extent, shards, -0.22, 0.18)
    return jnp.clip(drawn, -most, most).astype(held_as)


def noise_with(own_key, extent, deviation, limit, cuts, heavy, kind=jnp.bfloat16):
    values = deviation * jax.random.normal(own_key, extent, jnp.float32)
    if cuts:
        values = values * block_scale(own_key, extent, cuts, -0.22, 0.18)
    return jnp.clip(spiked(values, jax.random.fold_in(own_key, 3), *heavy), -limit, limit).astype(kind)


def setup_inputs(seed: int = 0) -> dict:
    streams_of = jax.random.split(jax.random.key(seed), 9)
    tokens = noise(streams_of[0], (TOKENS, D), 1.0, 6.0, ((0, 4), (1, 8)))
    cotangent = noise(streams_of[1], (TOKENS, D), 1.0, 6.0, ((0, 4), (1, 8)))
    gate_weight = noise_with(streams_of[2], (D, FF), (D // 2) ** -0.5, 0.1875, ((0, 4), (1, 8)), (1, 0, 8, 2.0))
    up_weight = noise_with(streams_of[3], (D, FF), (D // 2) ** -0.5, 0.1875, ((0, 4), (1, 8)), (1, 0, 8, 2.0))
    down_weight = noise_with(streams_of[4], (FF, D), (FF // 2) ** -0.5, 0.09375, ((0, 8), (1, 4)), (0, 1, 8, 2.0))
    gate_mask = draw_gate_mask(jax.random.fold_in(streams_of[8], 71), 0)
    up_mask = draw_up_mask(jax.random.fold_in(streams_of[8], 71), 0)
    down_mask = draw_down_mask(jax.random.fold_in(streams_of[8], 71), 0)
    return dict(tokens=tokens, cotangent=cotangent, gate_weight=gate_weight, up_weight=up_weight, down_weight=down_weight, gate_mask=gate_mask, up_mask=up_mask, down_mask=down_mask)


def masked(weight, block_mask):
    row_count, col_count = block_mask.shape
    shaped = weight.reshape(row_count, BLOCK, col_count, BLOCK)
    scaled = shaped * block_mask.astype(weight.dtype)[:, None, :, None]
    return scaled.reshape(weight.shape)


def reference(tokens, cotangent, gate_weight, up_weight, down_weight, gate_mask, up_mask, down_mask):
    gate_eff = masked(gate_weight, gate_mask)
    up_eff = masked(up_weight, up_mask)
    down_eff = masked(down_weight, down_mask)
    gate = jnp.dot(tokens, gate_eff, preferred_element_type=jnp.float32)
    up = jnp.dot(tokens, up_eff, preferred_element_type=jnp.float32)
    sigma = jax.nn.sigmoid(gate)
    silu_gate = gate * sigma
    hidden = (silu_gate * up).astype(jnp.bfloat16)
    grad_hidden = jnp.dot(cotangent, down_eff.T, preferred_element_type=jnp.float32)
    grad_gate = (grad_hidden * up * sigma * (1.0 + gate * (1.0 - sigma))).astype(jnp.bfloat16)
    grad_up = (grad_hidden * silu_gate).astype(jnp.bfloat16)
    span = FF // N_COL

    def add_group(carry, group):
        out_total, grad_total = carry
        start = group * span
        hidden_share = lax.dynamic_slice_in_dim(hidden, start, span, 1)
        down_rows = lax.dynamic_slice_in_dim(down_eff, start, span, 0)
        out_part = jnp.dot(hidden_share, down_rows, preferred_element_type=jnp.float32).astype(jnp.bfloat16)
        out_part = lax.optimization_barrier(out_part).astype(jnp.float32)
        gate_share = lax.dynamic_slice_in_dim(grad_gate, start, span, 1)
        up_share = lax.dynamic_slice_in_dim(grad_up, start, span, 1)
        gate_cols = lax.dynamic_slice_in_dim(gate_eff, start, span, 1)
        up_cols = lax.dynamic_slice_in_dim(up_eff, start, span, 1)
        grad_part = jnp.dot(gate_share, gate_cols.T, preferred_element_type=jnp.float32)
        grad_part = grad_part + jnp.dot(up_share, up_cols.T, preferred_element_type=jnp.float32)
        grad_part = lax.optimization_barrier(grad_part.astype(jnp.bfloat16)).astype(jnp.float32)
        return (out_total + out_part, grad_total + grad_part), None

    zeros = jnp.zeros(tokens.shape, jnp.float32)
    groups = jnp.arange(N_COL, dtype=jnp.int32)
    (out_total, grad_total), unused = lax.scan(add_group, (zeros, zeros), groups)
    return out_total.astype(jnp.bfloat16), grad_total.astype(jnp.bfloat16)
```

```python
import jax
import jax.numpy as jnp
from jax import lax
from jax.sharding import PartitionSpec as P

BLOCK = 128


def masked(weight, block_mask):
    rows, cols = block_mask.shape
    shaped = weight.reshape(rows, BLOCK, cols, BLOCK)
    return (shaped * block_mask.astype(weight.dtype)[:, None, :, None]).reshape(weight.shape)


def body(tokens, cotangent, gate_weight, up_weight, down_weight, gate_mask, up_mask, down_mask):
    rows, cols = lax.axis_size("row"), lax.axis_size("col")
    per = cols // rows
    perm = [
        (r * cols + j * per + h, j * cols + r * per + h)
        for r in range(rows)
        for j in range(rows)
        for h in range(per)
    ]
    local_tokens, local_features = tokens.shape
    shard = jnp.stack([tokens, cotangent])
    shard = lax.ppermute(shard, ("row", "col"), perm)
    panel = lax.all_gather(shard, "col", axis=0)
    panel = panel.reshape(rows, per, 2, local_tokens, local_features)
    panel = panel.transpose(2, 0, 3, 1, 4).reshape(2, rows * local_tokens, per * local_features)

    gate_eff = masked(gate_weight, gate_mask)
    up_eff = masked(up_weight, up_mask)
    down_eff = masked(down_weight, down_mask)

    contract = (((1,), (1,)), ((), ()))

    def reduced(part):
        return lax.psum_scatter(
            part.astype(jnp.bfloat16), "row", scatter_dimension=0, tiled=True
        ).astype(jnp.float32)

    gate = reduced(jnp.dot(panel[0], gate_eff, preferred_element_type=jnp.float32))
    up = reduced(jnp.dot(panel[0], up_eff, preferred_element_type=jnp.float32))
    grad_hidden = reduced(
        lax.dot_general(panel[1], down_eff, contract, preferred_element_type=jnp.float32)
    )
    sigma = jax.nn.sigmoid(gate)
    silu_gate = gate * sigma
    hidden = (silu_gate * up).astype(jnp.bfloat16)
    hidden = lax.all_gather(hidden, "row", axis=0, tiled=True)
    grad_gate = (grad_hidden * up * sigma * (1.0 + gate * (1.0 - sigma))).astype(jnp.bfloat16)
    grad_up = (grad_hidden * silu_gate).astype(jnp.bfloat16)
    grad_up = lax.all_gather(grad_up, "row", axis=0, tiled=True)
    grad_gate = lax.all_gather(grad_gate, "row", axis=0, tiled=True)

    out_part = jnp.dot(hidden, down_eff, preferred_element_type=jnp.float32)
    grad_part = lax.dot_general(grad_up, up_eff, contract, preferred_element_type=jnp.float32)
    grad_part = grad_part + lax.dot_general(
        grad_gate, gate_eff, contract, preferred_element_type=jnp.float32
    )

    def finish(part):
        part = part.astype(jnp.bfloat16).reshape(rows, local_tokens, per, local_features)
        part = part.transpose(0, 2, 1, 3).reshape(cols, local_tokens, local_features)
        part = lax.psum_scatter(part, "col", scatter_dimension=0, tiled=False)
        return lax.ppermute(part, ("row", "col"), perm)

    return finish(out_part), finish(grad_part)


def solution(mesh):
    in_specs = (
        P("row", "col"),
        P("row", "col"),
        P("row", "col"),
        P("row", "col"),
        P("col", "row"),
        P("row", "col"),
        P("row", "col"),
        P("col", "row"),
    )
    out_specs = (P("row", "col"), P("row", "col"))
    return jax.shard_map(body, mesh=mesh, in_specs=in_specs, out_specs=out_specs, check_vma=False)
```

```python
import functools

import jax
import jax.numpy as jnp
from jax import lax
from jax.experimental import pallas as pl
from jax.experimental.pallas import tpu as pltpu
from jax.sharding import PartitionSpec as P

BLOCK = 128
WIDTH = 128
LAG = 2
CONTRACT = (((1,), (1,)), ((), ()))


def masked(weight, block_mask):
    rows, cols = block_mask.shape
    shaped = weight.reshape(rows, BLOCK, cols, BLOCK)
    return (shaped * block_mask.astype(weight.dtype)[:, None, :, None]).reshape(weight.shape)


def chain_kernel(
    rows, per, x_ref, wg_ref, wu_ref, wd_ref, out_ref,
    part, hid, acc_out, acc_grad, tmp, rs_send, rs_recv, ag_send, ag_recv,
):
    me = lax.axis_index("row")
    last = rows - 1
    half = x_ref.shape[1] // 2
    chunks = wd_ref.shape[0] // WIDTH
    f32 = jnp.float32
    pos = (me, last - me)
    ahead = (jnp.minimum(me + 1, last), jnp.maximum(me - 1, 0))
    behind = (jnp.maximum(me - 1, 0), jnp.minimum(me + 1, last))

    barrier = pltpu.get_barrier_semaphore()

    @pl.when(me > 0)
    def _():
        pl.semaphore_signal(barrier, inc=1, device_id={"row": me - 1}, device_id_type=pl.DeviceIdType.MESH)

    @pl.when(me < last)
    def _():
        pl.semaphore_signal(barrier, inc=1, device_id={"row": me + 1}, device_id_type=pl.DeviceIdType.MESH)

    @pl.when((me > 0) & (me < last))
    def _():
        pl.semaphore_wait(barrier, 2)

    @pl.when((me == 0) | (me == last))
    def _():
        pl.semaphore_wait(barrier, 1)

    acc_out[...] = jnp.zeros_like(acc_out)
    acc_grad[...] = jnp.zeros_like(acc_grad)

    def rs_copy(d, k):
        return pltpu.make_async_remote_copy(
            src_ref=part.at[d, k], dst_ref=part.at[d, k],
            send_sem=rs_send.at[d, k], recv_sem=rs_recv.at[d, k],
            device_id={"row": ahead[d]}, device_id_type=pl.DeviceIdType.MESH,
        )

    def ag_copy(d, k):
        return pltpu.make_async_remote_copy(
            src_ref=hid.at[d, k], dst_ref=hid.at[d, k],
            send_sem=ag_send.at[d, k], recv_sem=ag_recv.at[d, k],
            device_id={"row": behind[d]}, device_id_type=pl.DeviceIdType.MESH,
        )

    def relay(d, k):
        @pl.when(pos[d] < last)
        def _():
            ag_copy(d, k).wait_recv()

            @pl.when(pos[d] > 0)
            def _():
                ag_copy(d, k).start()

    def reduce(d, k):
        span = pl.ds(pl.multiple_of(k * WIDTH, WIDTH), WIDTH)
        tok = x_ref[0, d * half : (d + 1) * half, :]
        cot = x_ref[1, d * half : (d + 1) * half, :]
        tmp[0] = jnp.dot(tok, wg_ref[:, span], preferred_element_type=f32)
        tmp[1] = jnp.dot(tok, wu_ref[:, span], preferred_element_type=f32)
        tmp[2] = lax.dot_general(cot, wd_ref[span, :], CONTRACT, preferred_element_type=f32)

        @pl.when(pos[d] == 0)
        def _():
            part[d, k] = tmp[...].astype(jnp.bfloat16)

        @pl.when(pos[d] > 0)
        def _():
            rs_copy(d, k).wait_recv()

        @pl.when((pos[d] > 0) & (pos[d] < last))
        def _():
            part[d, k] = (tmp[...] + part[d, k].astype(f32)).astype(jnp.bfloat16)

        @pl.when(pos[d] < last)
        def _():
            rs_copy(d, k).start()

        @pl.when(pos[d] == last)
        def _():
            gate = tmp[0] + part[d, k, 0].astype(f32)
            up = tmp[1] + part[d, k, 1].astype(f32)
            grad = tmp[2] + part[d, k, 2].astype(f32)
            sigma = jax.nn.sigmoid(gate)
            silu = gate * sigma
            hid[d, k, 0] = (silu * up).astype(jnp.bfloat16)
            hid[d, k, 1] = (grad * up * sigma * (1.0 + gate * (1.0 - sigma))).astype(jnp.bfloat16)
            hid[d, k, 2] = (grad * silu).astype(jnp.bfloat16)
            ag_copy(d, k).start()

    def expand(d, k):
        span = pl.ds(pl.multiple_of(k * WIDTH, WIDTH), WIDTH)
        acc_out[d] += jnp.dot(hid[d, k, 0], wd_ref[span, :], preferred_element_type=f32)
        acc_grad[d] += lax.dot_general(
            hid[d, k, 1], wg_ref[:, span], CONTRACT, preferred_element_type=f32
        ) + lax.dot_general(hid[d, k, 2], wu_ref[:, span], CONTRACT, preferred_element_type=f32)

    def guarded(fn, d, k):
        @pl.when((k >= 0) & (k < chunks))
        def _():
            fn(d, k)

    def step(s, carry):
        for d in range(2):
            guarded(relay, d, s - LAG * (2 * last - pos[d]))
        for d in range(2):
            guarded(reduce, d, s - LAG * pos[d])
        for d in range(2):
            guarded(expand, d, s - LAG * (2 * last - pos[d]))
        return carry

    lax.fori_loop(0, chunks + LAG * 2 * last, step, 0)

    tokens, features = out_ref.shape[2:]
    for j in range(rows):
        d, start = divmod(j * tokens, half)
        for h in range(per):
            cut = slice(h * features, (h + 1) * features)
            out_ref[j * per + h, 0] = acc_out[d, start : start + tokens, cut].astype(jnp.bfloat16)
            out_ref[j * per + h, 1] = acc_grad[d, start : start + tokens, cut].astype(jnp.bfloat16)

    def drain(k, carry):
        for d in range(2):
            @pl.when(pos[d] < last)
            def _():
                rs_copy(d, k).wait_send()

            @pl.when(pos[d] > 0)
            def _():
                ag_copy(d, k).wait_send()
        return carry

    lax.fori_loop(0, chunks, drain, 0)


def chain(rows, per, local_tokens, local_features, panel, gate_eff, up_eff, down_eff):
    tokens, features = panel.shape[1:]
    half = tokens // 2
    chunks = down_eff.shape[0] // WIDTH
    bf16, f32 = jnp.bfloat16, jnp.float32
    return pl.pallas_call(
        functools.partial(chain_kernel, rows, per),
        out_shape=jax.ShapeDtypeStruct((rows * per, 2, local_tokens, local_features), bf16),
        in_specs=[pl.BlockSpec(memory_space=pltpu.VMEM)] * 4,
        out_specs=pl.BlockSpec(memory_space=pltpu.VMEM),
        scratch_shapes=[
            pltpu.VMEM((2, chunks, 3, half, WIDTH), bf16),
            pltpu.VMEM((2, chunks, 3, half, WIDTH), bf16),
            pltpu.VMEM((2, half, features), f32),
            pltpu.VMEM((2, half, features), f32),
            pltpu.VMEM((3, half, WIDTH), f32),
            pltpu.SemaphoreType.DMA((2, chunks)),
            pltpu.SemaphoreType.DMA((2, chunks)),
            pltpu.SemaphoreType.DMA((2, chunks)),
            pltpu.SemaphoreType.DMA((2, chunks)),
        ],
        compiler_params=pltpu.CompilerParams(
            collective_id=0, has_side_effects=True, vmem_limit_bytes=56 * 1024 * 1024
        ),
        name="chain",
    )(panel, gate_eff, up_eff, down_eff)


def body(tokens, cotangent, gate_weight, up_weight, down_weight, gate_mask, up_mask, down_mask):
    rows, cols = lax.axis_size("row"), lax.axis_size("col")
    per = cols // rows
    perm = [
        (r * cols + j * per + h, j * cols + r * per + h)
        for r in range(rows)
        for j in range(rows)
        for h in range(per)
    ]
    local_tokens, local_features = tokens.shape
    shard = jnp.stack([tokens, cotangent])
    shard = lax.ppermute(shard, ("row", "col"), perm)
    panel = lax.all_gather(shard, "col", axis=0)
    panel = panel.reshape(rows, per, 2, local_tokens, local_features)
    panel = panel.transpose(2, 0, 3, 1, 4).reshape(2, rows * local_tokens, per * local_features)

    gate_eff = masked(gate_weight, gate_mask)
    up_eff = masked(up_weight, up_mask)
    down_eff = masked(down_weight, down_mask)

    part = chain(rows, per, local_tokens, local_features, panel, gate_eff, up_eff, down_eff)
    part = lax.psum_scatter(part, "col", scatter_dimension=0, tiled=False)
    part = lax.ppermute(part, ("row", "col"), perm)
    return part[0], part[1]


def solution(mesh):
    in_specs = (
        P("row", "col"),
        P("row", "col"),
        P("row", "col"),
        P("row", "col"),
        P("col", "row"),
        P("row", "col"),
        P("row", "col"),
        P("col", "row"),
    )
    out_specs = (P("row", "col"), P("row", "col"))
    return jax.shard_map(body, mesh=mesh, in_specs=in_specs, out_specs=out_specs, check_vma=False)
```

```python
import functools

import jax
import jax.numpy as jnp
from jax import lax
from jax.experimental import pallas as pl
from jax.experimental.pallas import tpu as pltpu
from jax.sharding import PartitionSpec as P

BLOCK = 128
WIDTH = 128
LAG = 2
CONTRACT = (((1,), (1,)), ((), ()))


def masked(weight, block_mask):
    rows, cols = block_mask.shape
    shaped = weight.reshape(rows, BLOCK, cols, BLOCK)
    return (shaped * block_mask.astype(weight.dtype)[:, None, :, None]).reshape(weight.shape)


def chain_kernel(
    rows, per, x_ref, wg_ref, wu_ref, wd_ref, out_ref,
    part, hid, acc_out, acc_grad, tmp, rs_send, rs_recv, ag_send, ag_recv,
):
    me = lax.axis_index("row")
    last = rows - 1
    half = x_ref.shape[1] // 2
    chunks = wd_ref.shape[0] // WIDTH
    f32 = jnp.float32
    pos = (me, last - me)
    ahead = (jnp.minimum(me + 1, last), jnp.maximum(me - 1, 0))
    behind = (jnp.maximum(me - 1, 0), jnp.minimum(me + 1, last))

    barrier = pltpu.get_barrier_semaphore()

    @pl.when(me > 0)
    def _():
        pl.semaphore_signal(barrier, inc=1, device_id={"row": me - 1}, device_id_type=pl.DeviceIdType.MESH)

    @pl.when(me < last)
    def _():
        pl.semaphore_signal(barrier, inc=1, device_id={"row": me + 1}, device_id_type=pl.DeviceIdType.MESH)

    @pl.when((me > 0) & (me < last))
    def _():
        pl.semaphore_wait(barrier, 2)

    @pl.when((me == 0) | (me == last))
    def _():
        pl.semaphore_wait(barrier, 1)

    acc_out[...] = jnp.zeros_like(acc_out)
    acc_grad[...] = jnp.zeros_like(acc_grad)

    def rs_copy(d, k):
        return pltpu.make_async_remote_copy(
            src_ref=part.at[d, k], dst_ref=part.at[d, k],
            send_sem=rs_send.at[d, k], recv_sem=rs_recv.at[d, k],
            device_id={"row": ahead[d]}, device_id_type=pl.DeviceIdType.MESH,
        )

    def ag_copy(d, k):
        return pltpu.make_async_remote_copy(
            src_ref=hid.at[d, k], dst_ref=hid.at[d, k],
            send_sem=ag_send.at[d, k], recv_sem=ag_recv.at[d, k],
            device_id={"row": behind[d]}, device_id_type=pl.DeviceIdType.MESH,
        )

    def relay(d, k):
        @pl.when(pos[d] < last)
        def _():
            ag_copy(d, k).wait_recv()

            @pl.when(pos[d] > 0)
            def _():
                ag_copy(d, k).start()

    def reduce(d, k):
        span = pl.ds(pl.multiple_of(k * WIDTH, WIDTH), WIDTH)
        tok = x_ref[0, d * half : (d + 1) * half, :]
        cot = x_ref[1, d * half : (d + 1) * half, :]
        tmp[0] = jnp.dot(tok, wg_ref[:, span], preferred_element_type=f32)
        tmp[1] = jnp.dot(tok, wu_ref[:, span], preferred_element_type=f32)
        tmp[2] = lax.dot_general(cot, wd_ref[span, :], CONTRACT, preferred_element_type=f32)

        @pl.when(pos[d] == 0)
        def _():
            part[d, k] = tmp[...].astype(jnp.bfloat16)

        @pl.when(pos[d] > 0)
        def _():
            rs_copy(d, k).wait_recv()

        @pl.when((pos[d] > 0) & (pos[d] < last))
        def _():
            part[d, k] = (tmp[...] + part[d, k].astype(f32)).astype(jnp.bfloat16)

        @pl.when(pos[d] < last)
        def _():
            rs_copy(d, k).start()

        @pl.when(pos[d] == last)
        def _():
            gate = tmp[0] + part[d, k, 0].astype(f32)
            up = tmp[1] + part[d, k, 1].astype(f32)
            grad = tmp[2] + part[d, k, 2].astype(f32)
            sigma = jax.nn.sigmoid(gate)
            silu = gate * sigma
            hid[d, k, 0] = (silu * up).astype(jnp.bfloat16)
            hid[d, k, 1] = (grad * up * sigma * (1.0 + gate * (1.0 - sigma))).astype(jnp.bfloat16)
            hid[d, k, 2] = (grad * silu).astype(jnp.bfloat16)
            ag_copy(d, k).start()

    def expand(d, k):
        span = pl.ds(pl.multiple_of(k * WIDTH, WIDTH), WIDTH)
        acc_out[d] += jnp.dot(hid[d, k, 0], wd_ref[span, :], preferred_element_type=f32)
        acc_grad[d] += lax.dot_general(
            hid[d, k, 1], wg_ref[:, span], CONTRACT, preferred_element_type=f32
        ) + lax.dot_general(hid[d, k, 2], wu_ref[:, span], CONTRACT, preferred_element_type=f32)

    def guarded(fn, d, k):
        @pl.when((k >= 0) & (k < chunks))
        def _():
            fn(d, k)

    def step(s, carry):
        for d in range(2):
            guarded(relay, d, s - LAG * (2 * last - pos[d]))
        for d in range(2):
            guarded(reduce, d, s - LAG * pos[d])
        for d in range(2):
            guarded(expand, d, s - LAG * (2 * last - pos[d]))
        return carry

    lax.fori_loop(0, chunks + LAG * 2 * last, step, 0)

    tokens, features = out_ref.shape[2:]
    for j in range(rows):
        d, start = divmod(j * tokens, half)
        for h in range(per):
            cut = slice(h * features, (h + 1) * features)
            out_ref[j * per + h, 0] = acc_out[d, start : start + tokens, cut].astype(jnp.bfloat16)
            out_ref[j * per + h, 1] = acc_grad[d, start : start + tokens, cut].astype(jnp.bfloat16)

    def drain(k, carry):
        for d in range(2):
            @pl.when(pos[d] < last)
            def _():
                rs_copy(d, k).wait_send()

            @pl.when(pos[d] > 0)
            def _():
                ag_copy(d, k).wait_send()
        return carry

    lax.fori_loop(0, chunks, drain, 0)


def chain(rows, per, local_tokens, local_features, panel, gate_eff, up_eff, down_eff):
    tokens, features = panel.shape[1:]
    half = tokens // 2
    chunks = down_eff.shape[0] // WIDTH
    bf16, f32 = jnp.bfloat16, jnp.float32
    return pl.pallas_call(
        functools.partial(chain_kernel, rows, per),
        out_shape=jax.ShapeDtypeStruct((rows * per, 2, local_tokens, local_features), bf16),
        in_specs=[pl.BlockSpec(memory_space=pltpu.VMEM)] * 4,
        out_specs=pl.BlockSpec(memory_space=pltpu.VMEM),
        scratch_shapes=[
            pltpu.VMEM((2, chunks, 3, half, WIDTH), bf16),
            pltpu.VMEM((2, chunks, 3, half, WIDTH), bf16),
            pltpu.VMEM((2, half, features), f32),
            pltpu.VMEM((2, half, features), f32),
            pltpu.VMEM((3, half, WIDTH), f32),
            pltpu.SemaphoreType.DMA((2, chunks)),
            pltpu.SemaphoreType.DMA((2, chunks)),
            pltpu.SemaphoreType.DMA((2, chunks)),
            pltpu.SemaphoreType.DMA((2, chunks)),
        ],
        compiler_params=pltpu.CompilerParams(
            collective_id=0, has_side_effects=True, vmem_limit_bytes=56 * 1024 * 1024
        ),
        name="chain",
    )(panel, gate_eff, up_eff, down_eff)


MESH_ID = pl.DeviceIdType.MESH


def meet(row, col, rows, cols, per):
    other_row, other_col = col // per, row * per + col % per
    away = other_row != row
    barrier = pltpu.get_barrier_semaphore()
    for off in range(1, cols):
        peer = lax.rem(col + off, cols)
        pl.semaphore_signal(barrier, inc=1, device_id={"row": row, "col": peer}, device_id_type=MESH_ID)

    @pl.when(away)
    def _():
        pl.semaphore_signal(
            barrier, inc=1, device_id={"row": other_row, "col": other_col}, device_id_type=MESH_ID
        )
        pl.semaphore_wait(barrier, cols)

    @pl.when(jnp.logical_not(away))
    def _():
        pl.semaphore_wait(barrier, cols - 1)

    return other_row, other_col, away


def spread_kernel(rows, cols, per, x_ref, out_ref, stage, swap_send, swap_recv, send, recv):
    row, col = lax.axis_index("row"), lax.axis_index("col")
    other_row, other_col, away = meet(row, col, rows, cols, per)

    @pl.when(away)
    def _():
        copy = pltpu.make_async_remote_copy(
            src_ref=x_ref, dst_ref=stage, send_sem=swap_send, recv_sem=swap_recv,
            device_id={"row": other_row, "col": other_col}, device_id_type=MESH_ID,
        )
        copy.start()
        copy.wait()

    @pl.when(jnp.logical_not(away))
    def _():
        copy = pltpu.make_async_copy(x_ref, stage, swap_send)
        copy.start()
        copy.wait()

    copies = []
    for off in range(1, cols):
        copy = pltpu.make_async_remote_copy(
            src_ref=stage, dst_ref=out_ref.at[col], send_sem=send.at[off], recv_sem=recv.at[off],
            device_id={"row": row, "col": lax.rem(col + off, cols)}, device_id_type=MESH_ID,
        )
        copy.start()
        copies.append(copy)
    out_ref[col] = stage[...]
    for off in range(1, cols):
        copies[off - 1].wait_send()
        origin = lax.rem(col + cols - off, cols)
        pltpu.make_async_remote_copy(
            src_ref=stage, dst_ref=out_ref.at[origin], send_sem=send.at[off], recv_sem=recv.at[off],
            device_id={"row": row, "col": origin}, device_id_type=MESH_ID,
        ).wait_recv()


def collect_kernel(rows, cols, per, p_ref, out_ref, land, total, swap_send, swap_recv, send, recv):
    row, col = lax.axis_index("row"), lax.axis_index("col")
    other_row, other_col, away = meet(row, col, rows, cols, per)
    copies = []
    for off in range(1, cols):
        peer = lax.rem(col + off, cols)
        copy = pltpu.make_async_remote_copy(
            src_ref=p_ref.at[peer], dst_ref=land.at[off - 1], send_sem=send.at[off], recv_sem=recv.at[off],
            device_id={"row": row, "col": peer}, device_id_type=MESH_ID,
        )
        copy.start()
        copies.append(copy)
    value = p_ref[col].astype(jnp.float32)
    for off in range(1, cols):
        copies[off - 1].wait()
        value = value + land[off - 1].astype(jnp.float32)
    total[...] = value.astype(total.dtype)

    @pl.when(away)
    def _():
        copy = pltpu.make_async_remote_copy(
            src_ref=total, dst_ref=out_ref, send_sem=swap_send, recv_sem=swap_recv,
            device_id={"row": other_row, "col": other_col}, device_id_type=MESH_ID,
        )
        copy.start()
        copy.wait()

    @pl.when(jnp.logical_not(away))
    def _():
        out_ref[...] = total[...]


def exchange(kernel, name, ident, rows, cols, per, value, out_shape, buffers):
    dma = pltpu.SemaphoreType.DMA
    return pl.pallas_call(
        functools.partial(kernel, rows, cols, per),
        out_shape=jax.ShapeDtypeStruct(out_shape, value.dtype),
        in_specs=[pl.BlockSpec(memory_space=pltpu.VMEM)],
        out_specs=pl.BlockSpec(memory_space=pltpu.VMEM),
        scratch_shapes=[pltpu.VMEM(shape, value.dtype) for shape in buffers]
        + [dma(()), dma(()), dma((cols,)), dma((cols,))],
        compiler_params=pltpu.CompilerParams(
            collective_id=ident, has_side_effects=True, vmem_limit_bytes=32 * 1024 * 1024
        ),
        name=name,
    )(value)


def body(tokens, cotangent, gate_weight, up_weight, down_weight, gate_mask, up_mask, down_mask):
    rows, cols = lax.axis_size("row"), lax.axis_size("col")
    per = cols // rows
    local_tokens, local_features = tokens.shape
    shard = jnp.stack([tokens, cotangent])
    panel = exchange(
        spread_kernel, "spread", 1, rows, cols, per, shard, (cols,) + shard.shape, [shard.shape]
    )
    panel = panel.reshape(rows, per, 2, local_tokens, local_features)
    panel = panel.transpose(2, 0, 3, 1, 4).reshape(2, rows * local_tokens, per * local_features)

    gate_eff = masked(gate_weight, gate_mask)
    up_eff = masked(up_weight, up_mask)
    down_eff = masked(down_weight, down_mask)

    part = chain(rows, per, local_tokens, local_features, panel, gate_eff, up_eff, down_eff)
    part = exchange(
        collect_kernel, "collect", 2, rows, cols, per, part, part.shape[1:],
        [(cols - 1,) + part.shape[1:], part.shape[1:]],
    )
    return part[0], part[1]


def solution(mesh):
    in_specs = (
        P("row", "col"),
        P("row", "col"),
        P("row", "col"),
        P("row", "col"),
        P("col", "row"),
        P("row", "col"),
        P("row", "col"),
        P("col", "row"),
    )
    out_specs = (P("row", "col"), P("row", "col"))
    return jax.shard_map(body, mesh=mesh, in_specs=in_specs, out_specs=out_specs, check_vma=False)
```
